128 devices in a mesh: dp: 16 (over z, y_lo, core), expert: 8 (over x, y_hi).
Axes of the slice: x: 4, y: 4 (y_hi: 2, y_lo: 2; y = y_hi * 2 + y_lo), z: 4, core: 2. Of those that a mesh axis runs over, the one named last changes fastest.
Arguments:
- tokens: bfloat16 [16384, 4096], P(('dp', 'expert')), may hold values from -6 to 6
- expert_ids: int32 [16384, 2], P(('dp', 'expert')), may hold values from 0 to 7, all different within a row; in each aligned block of 128 rows (0 to 127, 128 to 255, ...) at most 80 rows name the same one
- gate_probs: float32 [16384, 2], P(('dp', 'expert')), may hold values from 0.2 to 1
- gate_weight: bfloat16 [8, 4096, 1536], P('expert', 'dp'), may hold values from -0.09375 to 0.09375
- up_weight: bfloat16 [8, 4096, 1536], P('expert', 'dp'), may hold values from -0.09375 to 0.09375
- down_weight: bfloat16 [8, 1536, 4096], P('expert', None, 'dp'), may hold values from -0.15625 to 0.15625
Outputs:
- mixed: bfloat16 [16384, 4096], P(('dp', 'expert'))
The draws below stay inside these ranges and needn't reach their ends.
Inputs may be any that keep to these rules, and one draw needn't show every extreme that they name: `expert_ids`: each token names 2 different experts. Among the 128 tokens of one device (aligned blocks of rows), no expert is named by more than 80 tokens, and in every draw some expert is named by exactly 80 tokens of some device.
All inputs are finite; a program needn't handle non-finite values.
Results may differ from the reference program's by a relative error of at most 0.0057.
Values may be sent and summed in bfloat16 or wider, within the bound.
A program may use at most 128 MiB of HBM per device.

```python
import math
import jax
import jax.numpy as jnp
import numpy as np
from jax import lax

D = 4096
FF = 1536
TOP = 2
TOK_DEV = 128
EXPERTS = 8
CAP = 80
TOKENS = 16384
N_DP = 16
N_EXPERT = 8


def levels(own_key, dims, split, low, high):
    def one(dim, parts):
        heights = jax.random.uniform(jax.random.fold_in(jax.random.fold_in(own_key, 6), dim), (parts,), jnp.float32, low / len(split), high / len(split))
        return jnp.repeat(jnp.exp(heights), dims[dim] // parts).reshape((-1,) + (1,) * (len(dims) - dim - 1))

    factor_of = one(*split[0])
    for cut in split[1:]:
        factor_of = factor_of * one(*cut)
    return factor_of


def routed_block(key, own, number, rows, number_of, top, most, slope):
    sequence = jax.random.permutation(key, number_of)
    packed, usual = shares(number_of, rows * top, most, slope, True), shares(number_of, rows * top, most, slope, False)
    places = jnp.arange(number_of)

    def named(sizes, offset_by):
        used = int((sizes > 0).sum())
        fixed = max(1, used // 4)
        shifted = fixed + (places - fixed + offset_by * (used - fixed)) % max(1, number_of - fixed)
        return jnp.zeros((number_of,), jnp.int32).at[sequence[jnp.where(places < fixed, places, shifted)]].set(jnp.asarray(sizes, jnp.int32))

    sizes = jnp.where(number % 4 == 0, named(packed, number // 4), named(usual, number - number // 4 - 1))
    mixed = jax.random.permutation(jax.random.fold_in(own, 3), number_of)
    donor, sink = mixed[0:number_of // 2 * 2:2], mixed[1:number_of // 2 * 2:2]
    slack = jnp.minimum(sizes[donor] - 1, most - sizes[sink]) // 2
    slack = jnp.where((donor == sequence[0]) | (sink == sequence[0]) | (sizes[sink] == 0), 0, jnp.maximum(slack, 0))
    shifted = jax.random.randint(jax.random.fold_in(own, 4), (number_of // 2,), 0, 1 << 20) % (slack + 1)
    sizes = sizes.at[donor].add(-shifted).at[sink].add(shifted)
    labels = jnp.searchsorted(jnp.cumsum(sizes), jnp.arange(rows * top), side="right").astype(jnp.int32)
    grid = labels.reshape(top, rows).T
    grid = grid[jax.random.permutation(jax.random.fold_in(own, 1), rows)]
    offset_by = jax.random.randint(jax.random.fold_in(own, 2), (rows, 1), 0, top)
    return jnp.take_along_axis(grid, (jnp.arange(top)[None, :] + offset_by) % top, axis=1)


def shares(number_of, total, limit, skew, full):
    loads = [(1 << 20) // math.isqrt(standing ** skew) + 1 for standing in range(1, number_of + 1)]
    largest = limit if full else min(limit, max(-(-total // number_of), total * loads[0] // sum(loads)))
    least = 1 if total - largest >= number_of - 1 else 0
    holding, surplus = [largest] + [least] * (number_of - 1), total - largest - least * (number_of - 1)
    while surplus > 0:
        candidates = [i for i in range(1, number_of) if holding[i] < largest] or [i for i in range(1, number_of) if holding[i] < limit]
        pool, budget = sum([loads[i] for i in candidates]), surplus
        for i in candidates:
            extra = min(limit - holding[i], max(1, budget * loads[i] // pool), surplus)
            holding[i] = holding[i] + extra
            surplus = surplus - extra
    return np.array(holding)


def noise(key, shape, spread, limit, shards=(), kind=jnp.bfloat16):
    array = jax.random.normal(key, shape, jnp.float32) * spread
    if len(shards) > 0:
        array = levels(key, shape, shards, -0.22, 0.18) * array
    return jnp.clip(array, min=-limit, max=limit).astype(kind)


def setup_inputs(seed: int = 0) -> dict:
    key_list = jax.random.split(jax.random.key(seed), 7)
    tokens = noise(key_list[0], (TOKENS, D), 1.0, 6.0, ((0, 128),))
    expert_ids_keys = jax.random.split(jax.random.fold_in(key_list[1], 1), TOKENS // TOK_DEV)
    expert_ids_turns = jax.random.permutation(jax.random.fold_in(key_list[1], 3), TOKENS // TOK_DEV)
    expert_ids = jax.vmap(lambda own, number: routed_block(jax.random.fold_in(key_list[1], 2), own, number, TOK_DEV, EXPERTS, TOP, CAP, 2))(expert_ids_keys, expert_ids_turns).reshape((TOKENS, TOP))
    gate_probs = jnp.clip(0.2 + 0.8 * jax.random.uniform(key_list[2], (TOKENS, TOP), jnp.float32) ** levels(key_list[2], (TOKENS, TOP), ((0, 128),), -0.2, 0.2), 0.2, 1.0)
    gate_weight = noise(key_list[3], (EXPERTS, D, FF), D ** -0.5, 0.09375, ((0, 8), (1, 16)))
    up_weight = noise(key_list[4], (EXPERTS, D, FF), D ** -0.5, 0.09375, ((0, 8), (1, 16)))
    down_weight = noise(key_list[5], (EXPERTS, FF, D), FF ** -0.5, 0.15625, ((0, 8), (2, 16)))
    return dict(tokens=tokens, expert_ids=expert_ids, gate_probs=gate_probs, gate_weight=gate_weight, up_weight=up_weight, down_weight=down_weight)


def reference(tokens, expert_ids, gate_probs, gate_weight, up_weight, down_weight):
    tok_count = tokens.shape[0]
    top_count = expert_ids.shape[1]
    flat_ids = expert_ids.reshape(-1).astype(jnp.int32)
    flat_probs = gate_probs.reshape(-1)
    ordering = jnp.argsort(flat_ids, stable=True).astype(jnp.int32)
    expert_range = jnp.arange(EXPERTS, dtype=jnp.int32)
    tallies = jnp.sum((flat_ids[:, None] == expert_range[None, :]).astype(jnp.int32), axis=0).astype(jnp.int32)
    beginnings = (jnp.cumsum(tallies) - tallies).astype(jnp.int32)
    window = N_DP * N_EXPERT * CAP
    row_block = math.gcd(window, 512)
    block_count = window // row_block
    padded_order = jnp.concatenate([ordering, jnp.zeros((window,), jnp.int32)])

    def per_expert(mixed, expert):
        def per_block(mixed, block_index):
            def compute(mixed):
                first = (beginnings[expert] + block_index * row_block).astype(jnp.int32)
                picked = lax.dynamic_slice(padded_order, (first,), (row_block,))
                valid = block_index * row_block + jnp.arange(row_block, dtype=jnp.int32) < tallies[expert]
                token_rows = (picked // top_count).astype(jnp.int32)
                rows = tokens[token_rows]
                gate = jnp.dot(rows, gate_weight[expert], preferred_element_type=jnp.float32)
                upper = jnp.dot(rows, up_weight[expert], preferred_element_type=jnp.float32)
                hidden = (jax.nn.silu(gate) * upper).astype(jnp.bfloat16)
                outputs = jnp.dot(hidden, down_weight[expert], preferred_element_type=jnp.float32).astype(jnp.bfloat16)
                scale = jnp.where(valid, flat_probs[picked], jnp.zeros_like(flat_probs[picked]))
                return mixed.at[token_rows].add(scale[:, None] * outputs.astype(jnp.float32))
            return lax.cond(block_index * row_block < tallies[expert], compute, lambda unchanged: unchanged, mixed), None
        mixed, unused = lax.scan(per_block, mixed, jnp.arange(block_count, dtype=jnp.int32))
        return mixed, None

    mixed, unused = lax.scan(per_expert, jnp.zeros((tok_count, tokens.shape[1]), jnp.float32), expert_range)
    return mixed.astype(jnp.bfloat16)
```

```python
import jax
import jax.numpy as jnp
from jax import lax
from jax.experimental import pallas as pl
from jax.experimental.pallas import tpu as pltpu
from jax.sharding import PartitionSpec as P

CAP = 80
MESH = pl.DeviceIdType.MESH
COPIES = 120

def slot(dz, dy):
    return (dz % 4) * 2 + dy


def kernel(tok_hbm, meta_ref, gate_hbm, up_hbm, down_hbm, out_ref,
           gate_buf, up_buf, down_buf, gate_acc, up_acc, rows, hidden, own_tok, peer_tok, peer_meta,
           back, lanes, part_send, part_recv, mix, ssem, rsem, lsem):
    dp = lax.axis_index("dp")
    ex = lax.axis_index("expert")
    core, y, z = dp % 2, (dp // 2) % 2, dp // 4
    x, h = ex // 2, ex % 2

    def device(x_, h_, z_, y_, c_):
        return (z_ * 4 + y_ * 2 + c_, x_ * 2 + h_)

    z_up, z_down = device(x, h, (z + 1) % 4, y, core), device(x, h, (z + 3) % 4, y, core)
    y_in = device(x, h, z, 1 - y, core)
    sibling = device(x, h, z, y, 1 - core)
    y_out = device(x, 1 - h, z, 1 - y, core)
    x_by = [device((x + d) % 4, h, z, y, core) for d in range(4)]

    partners = (z_up, z_down, y_in, sibling, y_out, x_by[1], x_by[2], x_by[3])
    barrier = pltpu.get_barrier_semaphore()
    load_own = pltpu.make_async_copy(tok_hbm, own_tok.at[pl.ds(0, 128), :], lsem.at[3])
    load_own.start()
    for partner in partners:
        pl.semaphore_signal(barrier, inc=1, device_id=partner, device_id_type=MESH)
    pl.semaphore_wait(barrier, len(partners))

    sends = []

    def send(src, dst, dev):
        i = len(sends)
        copy = pltpu.make_async_remote_copy(
            src_ref=src, dst_ref=dst, send_sem=ssem.at[i], recv_sem=rsem.at[i],
            device_id=dev, device_id_type=MESH)
        copy.start()
        sends.append(copy)
        return i

    def arrive(i, dst):
        pltpu.make_async_remote_copy(
            src_ref=dst, dst_ref=dst, send_sem=ssem.at[i], recv_sem=rsem.at[i],
            device_id=sibling, device_id_type=MESH).wait_recv()

    args = (gate_hbm.at[0], up_hbm.at[0], down_hbm.at[0])
    bufs = (gate_buf, up_buf, down_buf)
    sizes = (256, 256, 1536)
    extra = (48, 48, 256)
    events = {}
    local = []

    def span(ref, lo, hi):
        return ref.at[pl.ds(lo, hi - lo), :]

    def push(m, key, src, r, lo, hi, dev):
        i = send(span(src, lo, hi), span(bufs[m].at[r, core], lo, hi), dev)
        events[m, key] = (i, r, lo, hi)

    def take(m, key, who):
        i, r, lo, hi = events[m, key]
        arrive(i, span(bufs[m].at[r, who], lo, hi))

    def pass_on(m, key):
        i, r, lo, hi = events[m, key]
        take(m, key, core)
        push(m, "s" + key, bufs[m].at[r, core], r, lo, hi, sibling)

    def start_own(m):
        n = sizes[m]
        push(m, "y", args[m], slot(0, 1), 0, n, y_in)
        push(m, "zu", args[m], slot(3, 0), 0, n, z_up)
        push(m, "zd", args[m], slot(1, 0), 0, n, z_down)
        push(m, "sown", args[m], slot(0, 0), 0, n, sibling)
        copy = pltpu.make_async_copy(args[m], bufs[m].at[slot(0, 0), core], lsem.at[m])
        copy.start()
        local.append(copy)

    def hop_two(m):
        n = sizes[m]
        cut = n - extra[m]
        for key, dz, lo, hi, dev in (("zu", 3, 0, n // 2, z_up), ("zd", 1, n // 2, n, z_down)):
            take(m, key, core)
            src = bufs[m].at[slot(dz, 0), core]
            push(m, "2" + key, src, slot(2, 0), lo, hi, dev)
            push(m, "q" + key, src, slot(dz, 1), cut, n, y_in)
            push(m, "s" + key, src, slot(dz, 0), 0, n, sibling)
        take(m, "y", core)
        src = bufs[m].at[slot(0, 1), core]
        push(m, "yzu", src, slot(3, 1), 0, cut, z_up)
        push(m, "yzd", src, slot(1, 1), 0, cut, z_down)
        push(m, "sy", src, slot(0, 1), 0, n, sibling)

    def hop_three(m):
        for key in ("2zu", "2zd"):
            i, r, lo, hi = events[m, key]
            take(m, key, core)
            push(m, "y" + key, bufs[m].at[r, core], slot(2, 1), lo, hi, y_in)
            push(m, "s" + key, bufs[m].at[r, core], r, lo, hi, sibling)
        for key in ("qzu", "qzd", "yzu", "yzd"):
            pass_on(m, key)

    def hop_four(m):
        pass_on(m, "y2zu")
        pass_on(m, "y2zd")

    from_sibling = {
        slot(0, 0): ("sown",), slot(0, 1): ("sy",), slot(3, 0): ("szu",), slot(1, 0): ("szd",),
        slot(2, 0): ("s2zu", "s2zd"), slot(3, 1): ("sqzu", "syzu"), slot(1, 1): ("sqzd", "syzd"),
        slot(2, 1): ("sy2zu", "sy2zd")}

    def whole_slot(m, r):
        if r == slot(0, 0):
            local[m].wait()
        for key in from_sibling[r]:
            take(m, key, 1 - core)

    later = (lax.broadcasted_iota(jnp.int32, (128, 128), 0)
             < lax.broadcasted_iota(jnp.int32, (128, 128), 1)).astype(jnp.bfloat16)
    place = lax.broadcasted_iota(jnp.int32, (CAP, 128), 0).astype(jnp.float32)
    ahead = (lax.broadcasted_iota(jnp.int32, (8, 128), 0) + 1) % 4
    experts = (((x + ahead) % 4) * 2 + h).astype(jnp.float32)

    def route(meta):
        first, second = meta[0:1, :] == experts, meta[1:2, :] == experts
        named = jnp.where(first | second, 1.0, 0.0)
        weight = jnp.where(first, meta[2:3, :], 0.0) + jnp.where(second, meta[3:4, :], 0.0)
        rank = jnp.dot(named.astype(jnp.bfloat16), later, preferred_element_type=jnp.float32)
        picks = [jnp.where(place == rank[b:b + 1, :], named[b:b + 1, :], 0.0) for b in range(4)]
        return picks, [picks[b] * weight[b:b + 1, :] for b in range(4)]

    def dispatch(part, picks, source):
        chosen = jnp.concatenate(picks, axis=0).astype(jnp.bfloat16)

        def block(j, carry):
            cols = pl.ds(pl.multiple_of(j * 512, 512), 512)
            got = jnp.dot(chosen, source[pl.ds(0, 128), cols], preferred_element_type=jnp.float32).astype(jnp.bfloat16)
            for b in range(3):
                lanes[j, pl.ds(b * 160 + part * CAP, CAP), :] = got[b * CAP:(b + 1) * CAP]
            rows[j, pl.ds(480 + part * CAP, CAP), :] = got[3 * CAP:]
            return carry

        lax.fori_loop(0, 8, block, 0)
        ids = []
        for b in (0, 2, 1):
            at = pl.ds(b * 160 + part * CAP, CAP)
            ids.append((send(lanes.at[:, at, :], rows.at[:, at, :], x_by[b + 1]), at))
        return ids

    def block_of(r):
        return ((z + r // 2) % 4) * 2 + (y + r % 2) % 2

    def project(r, first, last):
        whole_slot(0, r)
        whole_slot(1, r)
        chip = block_of(r)

        def tile(n, carry):
            cols = pl.ds(pl.multiple_of(n * 256, 256), 256)
            seen = rows[chip]
            g = jnp.dot(seen, gate_buf[r, :, :, cols].reshape(512, 256), preferred_element_type=jnp.float32)
            u = jnp.dot(seen, up_buf[r, :, :, cols].reshape(512, 256), preferred_element_type=jnp.float32)
            if not first:
                g = gate_acc[:, cols] + g
                u = up_acc[:, cols] + u
            if last:
                hidden[:, cols] = (g / (1.0 + jnp.exp(-g)) * u).astype(jnp.bfloat16)
            else:
                gate_acc[:, cols] = g
                up_acc[:, cols] = u
            return carry

        lax.fori_loop(0, 6, tile, 0)

    homes = (own_tok, peer_tok, back)
    returns = {}

    def expand(g):
        whole_slot(2, g)

        def half(n, carry):
            cols = pl.ds(pl.multiple_of(n * 256, 256), 256)
            rows[g, :, cols] = jnp.dot(
                hidden[...], down_buf[g, n], preferred_element_type=jnp.float32).astype(jnp.bfloat16)
            return carry

        lax.fori_loop(0, 2, half, 0)
        returns[g] = []
        for b in (0, 2, 1):
            dst = homes[b].at[:, pl.ds(g * 512, 512)]
            returns[g].append((send(rows.at[g, pl.ds(b * 160, 160), :], dst, x_by[3 - b]), dst))

    parts = {}

    def combine(g):
        for i, dst in returns[g]:
            arrive(i, dst)
        total = 0.0
        for b in range(4):
            block = homes[b][:, pl.ds(g * 512, 512)] if b < 3 else rows[g, pl.ds(480, 160), :]
            for half in range(2):
                total = total + jnp.dot(mix[b, half], block, preferred_element_type=jnp.float32)
        gate_acc[pl.ds((g // 2) * 128, 128), pl.ds((g % 2) * 512, 512)] = total[:128]
        part_send[g] = total[128:].astype(jnp.bfloat16)
        parts[g] = send(part_send.at[g], part_recv.at[g ^ 1], y_out)

    def finish(g):
        arrive(parts[g ^ 1], part_recv.at[g])
        cols = pl.ds(pl.multiple_of(block_of(g) * 512, 512), 512)
        kept = gate_acc[pl.ds((g // 2) * 128, 128), pl.ds((g % 2) * 512, 512)]
        out_ref[:, cols] = (kept + part_recv[g].astype(jnp.float32)).astype(jnp.bfloat16)

    meta_id = send(meta_ref, peer_meta, y_out)
    tok_id = send(tok_hbm, peer_tok.at[pl.ds(0, 128), :], y_out)
    start_own(0)
    start_own(1)
    load_own.wait()
    picks, weighed = route(meta_ref[...])
    dispatched = dispatch(0, picks, own_tok)
    hop_two(0)
    arrive(meta_id, peer_meta)
    arrive(tok_id, peer_tok.at[pl.ds(0, 128), :])
    peer_picks, peer_weighed = route(peer_meta[...])
    dispatched += dispatch(1, peer_picks, peer_tok)
    hop_two(1)
    nothing = jnp.zeros((CAP, 128), jnp.float32)

    for b in range(4):
        whole = jnp.concatenate(
            [jnp.concatenate([weighed[b], nothing], axis=1),
             jnp.concatenate([nothing, peer_weighed[b]], axis=1)], axis=0).T
        high = whole.astype(jnp.bfloat16)
        mix[b, 0] = high
        mix[b, 1] = (whole - high.astype(jnp.float32)).astype(jnp.bfloat16)
    hop_three(0)
    start_own(2)
    hop_three(1)
    hop_four(0)
    for i, at in dispatched:
        arrive(i, rows.at[:, at, :])
    project(slot(0, 0), True, False)
    project(slot(0, 1), False, False)
    hop_two(2)
    hop_four(1)
    for r in (slot(3, 0), slot(1, 0), slot(2, 0), slot(3, 1), slot(1, 1)):
        project(r, False, False)
    project(slot(2, 1), False, True)
    expand(slot(0, 0))
    expand(slot(0, 1))
    hop_three(2)
    expand(slot(3, 0))
    expand(slot(1, 0))
    combine(slot(0, 0))
    expand(slot(2, 0))
    combine(slot(0, 1))
    expand(slot(3, 1))
    expand(slot(1, 1))
    combine(slot(3, 0))
    hop_four(2)
    expand(slot(2, 1))
    for g in (slot(1, 0), slot(2, 0), slot(3, 1), slot(1, 1), slot(2, 1)):
        combine(g)
    for g in (slot(0, 0), slot(0, 1), slot(3, 0), slot(1, 0), slot(2, 0), slot(3, 1), slot(1, 1), slot(2, 1)):
        finish(g)
    for copy in sends:
        copy.wait_send()


def on_device(tokens, expert_ids, gate_probs, gate_weight, up_weight, down_weight):
    meta = jnp.concatenate(
        [expert_ids.T.astype(jnp.float32), gate_probs.T, jnp.zeros((4, 128), jnp.float32)], axis=0)
    hbm, vmem = pl.BlockSpec(memory_space=pltpu.HBM), pl.BlockSpec(memory_space=pltpu.VMEM)
    return pl.pallas_call(
        kernel,
        out_shape=jax.ShapeDtypeStruct((128, 4096), jnp.bfloat16),
        in_specs=[hbm, vmem, hbm, hbm, hbm],
        out_specs=vmem,
        scratch_shapes=[
            pltpu.VMEM((8, 2, 256, 1536), jnp.bfloat16),
            pltpu.VMEM((8, 2, 256, 1536), jnp.bfloat16),
            pltpu.VMEM((8, 2, 1536, 256), jnp.bfloat16),
            pltpu.VMEM((640, 1536), jnp.float32),
            pltpu.VMEM((640, 1536), jnp.float32),
            pltpu.VMEM((8, 640, 512), jnp.bfloat16),
            pltpu.VMEM((640, 1536), jnp.bfloat16),
            pltpu.VMEM((160, 4096), jnp.bfloat16),
            pltpu.VMEM((160, 4096), jnp.bfloat16),
            pltpu.VMEM((8, 128), jnp.float32),
            pltpu.VMEM((160, 4096), jnp.bfloat16),
            pltpu.VMEM((8, 480, 512), jnp.bfloat16),
            pltpu.VMEM((8, 128, 512), jnp.bfloat16),
            pltpu.VMEM((8, 128, 512), jnp.bfloat16),
            pltpu.VMEM((4, 2, 256, 160), jnp.bfloat16),
            pltpu.SemaphoreType.DMA((COPIES,)),
            pltpu.SemaphoreType.DMA((COPIES,)),
            pltpu.SemaphoreType.DMA((4,)),
        ],
        compiler_params=pltpu.CompilerParams(
            collective_id=0, has_side_effects=True, vmem_limit_bytes=63 * 2**20),
        name="experts",
    )(tokens, meta, gate_weight, up_weight, down_weight)


def solution(mesh):
    placed = (
        P(("dp", "expert"), None),
        P(("dp", "expert"), None),
        P(("dp", "expert"), None),
        P("expert", "dp", None),
        P("expert", "dp", None),
        P("expert", None, "dp"),
    )
    return jax.shard_map(
        on_device, mesh=mesh, in_specs=placed, out_specs=P(("dp", "expert"), None), check_vma=False
    )
```

```python
import jax
import jax.numpy as jnp
from jax import lax
from jax.experimental import pallas as pl
from jax.experimental.pallas import tpu as pltpu
from jax.sharding import PartitionSpec as P

CAP = 80
MESH = pl.DeviceIdType.MESH
COPIES = 120

def slot(dz, dy):
    return (dz % 4) * 2 + dy


def kernel(tok_hbm, meta_ref, gate_hbm, up_hbm, down_hbm, out_ref,
           gate_buf, up_buf, down_buf, gate_acc, up_acc, rows, hidden, own_tok, peer_tok, peer_meta,
           back, lanes, part_recv, mix, ssem, rsem, lsem):
    dp = lax.axis_index("dp")
    ex = lax.axis_index("expert")
    core, y, z = dp % 2, (dp // 2) % 2, dp // 4
    x, h = ex // 2, ex % 2

    def device(x_, h_, z_, y_, c_):
        return (z_ * 4 + y_ * 2 + c_, x_ * 2 + h_)

    z_up, z_down = device(x, h, (z + 1) % 4, y, core), device(x, h, (z + 3) % 4, y, core)
    y_in = device(x, h, z, 1 - y, core)
    sibling = device(x, h, z, y, 1 - core)
    y_out = device(x, 1 - h, z, 1 - y, core)
    x_by = [device((x + d) % 4, h, z, y, core) for d in range(4)]

    partners = (z_up, z_down, y_in, sibling, y_out, x_by[1], x_by[2], x_by[3])
    barrier = pltpu.get_barrier_semaphore()
    load_own = pltpu.make_async_copy(tok_hbm, own_tok.at[pl.ds(0, 128), :], lsem.at[3])
    load_own.start()
    for partner in partners:
        pl.semaphore_signal(barrier, inc=1, device_id=partner, device_id_type=MESH)
    pl.semaphore_wait(barrier, len(partners))

    sends = []
    left = set()

    def send(src, dst, dev):
        i = len(sends)
        copy = pltpu.make_async_remote_copy(
            src_ref=src, dst_ref=dst, send_sem=ssem.at[i], recv_sem=rsem.at[i],
            device_id=dev, device_id_type=MESH)
        copy.start()
        sends.append(copy)
        return i

    def arrive(i, dst):
        pltpu.make_async_remote_copy(
            src_ref=dst, dst_ref=dst, send_sem=ssem.at[i], recv_sem=rsem.at[i],
            device_id=sibling, device_id_type=MESH).wait_recv()

    args = (gate_hbm.at[0], up_hbm.at[0], down_hbm.at[0])
    bufs = (gate_buf, up_buf, down_buf)
    sizes = (256, 256, 1536)
    extra = (48, 48, 256)
    events = {}
    local = []

    def span(ref, lo, hi):
        return ref.at[pl.ds(lo, hi - lo), :]

    def push(m, key, src, r, lo, hi, dev):
        i = send(span(src, lo, hi), span(bufs[m].at[r, core], lo, hi), dev)
        events[m, key] = (i, r, lo, hi)

    def take(m, key, who):
        i, r, lo, hi = events[m, key]
        arrive(i, span(bufs[m].at[r, who], lo, hi))

    def pass_on(m, key):
        i, r, lo, hi = events[m, key]
        take(m, key, core)
        push(m, "s" + key, bufs[m].at[r, core], r, lo, hi, sibling)

    def send_own(m, key):
        r, dev = {"y": (slot(0, 1), y_in), "zu": (slot(3, 0), z_up), "zd": (slot(1, 0), z_down)}[key]
        push(m, key, args[m], r, 0, sizes[m], dev)

    def keep_own(m):
        push(m, "sown", args[m], slot(0, 0), 0, sizes[m], sibling)

    for m in range(3):
        copy = pltpu.make_async_copy(args[m], bufs[m].at[slot(0, 0), core], lsem.at[m])
        copy.start()
        local.append(copy)

    def relay_half(m, key):
        n = sizes[m]
        dz, lo, hi, dev = {"zu": (3, 0, n // 2, z_up), "zd": (1, n // 2, n, z_down)}[key]
        take(m, key, core)
        src = bufs[m].at[slot(dz, 0), core]
        push(m, "2" + key, src, slot(2, 0), lo, hi, dev)
        push(m, "q" + key, src, slot(dz, 1), n - extra[m], n, y_in)
        push(m, "s" + key, src, slot(dz, 0), 0, n, sibling)

    def relay_peer(m):
        n = sizes[m]
        take(m, "y", core)
        src = bufs[m].at[slot(0, 1), core]
        push(m, "yzu", src, slot(3, 1), 0, n - extra[m], z_up)
        push(m, "yzd", src, slot(1, 1), 0, n - extra[m], z_down)
        push(m, "sy", src, slot(0, 1), 0, n, sibling)

    def relay_far(m, key):
        i, r, lo, hi = events[m, key]
        take(m, key, core)
        push(m, "y" + key, bufs[m].at[r, core], slot(2, 1), lo, hi, y_in)
        push(m, "s" + key, bufs[m].at[r, core], r, lo, hi, sibling)

    from_sibling = {
        slot(0, 0): ("sown",), slot(0, 1): ("sy",), slot(3, 0): ("szu",), slot(1, 0): ("szd",),
        slot(2, 0): ("s2zu", "s2zd"), slot(3, 1): ("sqzu", "syzu"), slot(1, 1): ("sqzd", "syzd"),
        slot(2, 1): ("sy2zu", "sy2zd")}

    def whole_slot(m, r):
        if r == slot(0, 0):
            local[m].wait()
        for key in from_sibling[r]:
            take(m, key, 1 - core)

    later = (lax.broadcasted_iota(jnp.int32, (128, 128), 0)
             < lax.broadcasted_iota(jnp.int32, (128, 128), 1)).astype(jnp.bfloat16)
    place = lax.broadcasted_iota(jnp.int32, (CAP, 128), 0).astype(jnp.float32)
    ahead = (lax.broadcasted_iota(jnp.int32, (8, 128), 0) + 1) % 4
    experts = (((x + ahead) % 4) * 2 + h).astype(jnp.float32)

    def route(meta):
        first, second = meta[0:1, :] == experts, meta[1:2, :] == experts
        named = jnp.where(first | second, 1.0, 0.0)
        weight = jnp.where(first, meta[2:3, :], 0.0) + jnp.where(second, meta[3:4, :], 0.0)
        rank = jnp.dot(named.astype(jnp.bfloat16), later, preferred_element_type=jnp.float32)
        picks = [jnp.where(place == rank[b:b + 1, :], named[b:b + 1, :], 0.0) for b in range(4)]
        return picks, [picks[b] * weight[b:b + 1, :] for b in range(4)]

    def dispatch(part, picks, source):
        chosen = jnp.concatenate(picks, axis=0).astype(jnp.bfloat16)

        def block(j, carry):
            cols = pl.ds(pl.multiple_of(j * 512, 512), 512)
            got = jnp.dot(chosen, source[pl.ds(0, 128), cols], preferred_element_type=jnp.float32).astype(jnp.bfloat16)
            for b in range(3):
                lanes[j, pl.ds(b * 160 + part * CAP, CAP), :] = got[b * CAP:(b + 1) * CAP]
            rows[j, pl.ds(480 + part * CAP, CAP), :] = got[3 * CAP:]
            return carry

        lax.fori_loop(0, 8, block, 0)
        ids = []
        for b in (0, 2, 1):
            at = pl.ds(b * 160 + part * CAP, CAP)
            ids.append((send(lanes.at[:, at, :], rows.at[:, at, :], x_by[b + 1]), at))
        return ids

    def block_of(r):
        return ((z + r // 2) % 4) * 2 + (y + r % 2) % 2

    accs = (gate_acc, up_acc)

    def clear():
        gate_acc[...] = jnp.zeros_like(gate_acc)
        up_acc[...] = jnp.zeros_like(up_acc)

    def project(m, r):
        whole_slot(m, r)
        chip = block_of(r)
        for n in range(2):
            at = pl.ds(n * 320, 320)
            accs[m][at, :] += jnp.dot(
                rows[chip, at, :], bufs[m][r].reshape(512, 1536), preferred_element_type=jnp.float32)

    def project_last(r):
        whole_slot(1, r)

        def tile(n, carry):
            cols = pl.ds(pl.multiple_of(n * 512, 512), 512)
            got = jnp.dot(
                rows[block_of(r)], up_buf[r, :, :, cols].reshape(512, 512), preferred_element_type=jnp.float32)
            hidden[:, cols] = (gate_acc[:, cols] * (up_acc[:, cols] + got)).astype(jnp.bfloat16)
            return carry

        lax.fori_loop(0, 3, tile, 0)

    def activate():
        def tile(n, carry):
            at = pl.ds(pl.multiple_of(n * 32, 32), 32)
            g = gate_acc[at, :]
            gate_acc[at, :] = g / (1.0 + jnp.exp(-g))
            return carry

        lax.fori_loop(0, 20, tile, 0)

    homes = (own_tok, peer_tok, back)
    returns = {}

    def expand(g):
        whole_slot(2, g)

        for n in range(2):
            rows[g, :, pl.ds(n * 256, 256)] = jnp.dot(
                hidden[...], down_buf[g, n], preferred_element_type=jnp.float32).astype(jnp.bfloat16)
        returns[g] = []
        for b in (0, 2, 1):
            dst = homes[b].at[:, pl.ds(g * 512, 512)]
            returns[g].append((send(rows.at[g, pl.ds(b * 160, 160), :], dst, x_by[3 - b]), dst))

    parts = {}
    dispatched = []

    def combine(g):
        for i, dst in returns[g]:
            arrive(i, dst)
        total = 0.0
        for b in range(4):
            block = homes[b][:, pl.ds(g * 512, 512)] if b < 3 else rows[g, pl.ds(480, 160), :]
            for half in range(2):
                total = total + jnp.dot(mix[b, half], block, preferred_element_type=jnp.float32)
        gate_acc[pl.ds((g // 2) * 128, 128), pl.ds((g % 2) * 512, 512)] = total[:128]
        if not parts:
            for i, at in dispatched:
                sends[i].wait_send()
                left.add(i)
        lanes[g, pl.ds(0, 128), :] = total[128:].astype(jnp.bfloat16)
        parts[g] = send(lanes.at[g, pl.ds(0, 128), :], part_recv.at[g ^ 1], y_out)

    def finish(g):
        arrive(parts[g ^ 1], part_recv.at[g])
        cols = pl.ds(pl.multiple_of(block_of(g) * 512, 512), 512)
        kept = gate_acc[pl.ds((g // 2) * 128, 128), pl.ds((g % 2) * 512, 512)]
        out_ref[:, cols] = (kept + part_recv[g].astype(jnp.float32)).astype(jnp.bfloat16)

    def set_mix(weighed, peer_weighed):
        nothing = jnp.zeros((CAP, 128), jnp.float32)
        for b in range(4):
            whole = jnp.concatenate(
                [jnp.concatenate([weighed[b], nothing], axis=1),
                 jnp.concatenate([nothing, peer_weighed[b]], axis=1)], axis=0).T
            high = whole.astype(jnp.bfloat16)
            mix[b, 0] = high
            mix[b, 1] = (whole - high.astype(jnp.float32)).astype(jnp.bfloat16)

    here, across, up1, down1 = slot(0, 0), slot(0, 1), slot(3, 0), slot(1, 0)
    far, up2, down2, far2 = slot(2, 0), slot(3, 1), slot(1, 1), slot(2, 1)

    meta_id = send(meta_ref, peer_meta, y_out)
    tok_id = send(tok_hbm, peer_tok.at[pl.ds(0, 128), :], y_out)
    send_own(0, "zd")
    send_own(0, "zu")
    send_own(1, "y")
    load_own.wait()
    picks, weighed = route(meta_ref[...])
    dispatched += dispatch(0, picks, own_tok)
    clear()
    send_own(1, "zd")
    send_own(0, "y")
    keep_own(1)
    send_own(1, "zu")
    relay_half(0, "zd")
    relay_half(0, "zu")
    relay_half(1, "zu")
    arrive(meta_id, peer_meta)
    arrive(tok_id, peer_tok.at[pl.ds(0, 128), :])
    peer_picks, peer_weighed = route(peer_meta[...])
    dispatched += dispatch(1, peer_picks, peer_tok)
    set_mix(weighed, peer_weighed)
    relay_half(1, "zd")
    relay_far(0, "2zd")
    relay_peer(0)
    pass_on(0, "qzu")
    relay_far(0, "2zu")
    relay_far(1, "2zd")
    relay_peer(1)
    keep_own(2)
    keep_own(0)
    for i, at in dispatched:
        arrive(i, rows.at[:, at, :])
    relay_far(1, "2zu")
    project(0, here)
    project(1, far)
    pass_on(0, "y2zu")
    project(1, up1)
    project(1, across)
    pass_on(1, "qzd")
    project(0, up1)
    project(1, down1)
    pass_on(0, "yzd")
    pass_on(0, "yzu")
    send_own(2, "zd")
    project(1, here)
    pass_on(1, "y2zd")
    send_own(2, "y")
    pass_on(0, "qzd")
    pass_on(0, "y2zd")
    pass_on(1, "qzu")
    project(0, far)
    project(0, up2)
    send_own(2, "zu")
    project(0, across)
    project(0, down2)
    project(0, far2)
    pass_on(1, "y2zu")
    project(0, down1)
    pass_on(1, "yzu")
    pass_on(1, "yzd")
    project(1, far2)
    project(1, up2)
    activate()
    project_last(down2)
    expand(here)
    relay_half(2, "zd")
    relay_half(2, "zu")
    relay_peer(2)
    expand(down1)
    expand(up1)
    relay_far(2, "2zd")
    expand(across)
    relay_far(2, "2zu")
    pass_on(2, "yzd")
    expand(far)
    combine(across)
    pass_on(2, "qzd")
    pass_on(2, "qzu")
    expand(down2)
    pass_on(2, "y2zu")
    combine(down1)
    pass_on(2, "y2zd")
    combine(far)
    combine(here)
    combine(up1)
    expand(far2)
    pass_on(2, "yzu")
    combine(down2)
    expand(up2)
    finish(here)
    finish(down1)
    combine(far2)
    finish(across)
    combine(up2)
    finish(down2)
    finish(up2)
    finish(far)
    finish(far2)
    finish(up1)
    for i, copy in enumerate(sends):
        if i not in left:
            copy.wait_send()


def on_device(tokens, expert_ids, gate_probs, gate_weight, up_weight, down_weight):
    meta = jnp.concatenate(
        [expert_ids.T.astype(jnp.float32), gate_probs.T, jnp.zeros((4, 128), jnp.float32)], axis=0)
    hbm, vmem = pl.BlockSpec(memory_space=pltpu.HBM), pl.BlockSpec(memory_space=pltpu.VMEM)
    return pl.pallas_call(
        kernel,
        out_shape=jax.ShapeDtypeStruct((128, 4096), jnp.bfloat16),
        in_specs=[hbm, vmem, hbm, hbm, hbm],
        out_specs=vmem,
        scratch_shapes=[
            pltpu.VMEM((8, 2, 256, 1536), jnp.bfloat16),
            pltpu.VMEM((8, 2, 256, 1536), jnp.bfloat16),
            pltpu.VMEM((8, 2, 1536, 256), jnp.bfloat16),
            pltpu.VMEM((640, 1536), jnp.float32),
            pltpu.VMEM((640, 1536), jnp.float32),
            pltpu.VMEM((8, 640, 512), jnp.bfloat16),
            pltpu.VMEM((640, 1536), jnp.bfloat16),
            pltpu.VMEM((160, 4096), jnp.bfloat16),
            pltpu.VMEM((160, 4096), jnp.bfloat16),
            pltpu.VMEM((8, 128), jnp.float32),
            pltpu.VMEM((160, 4096), jnp.bfloat16),
            pltpu.VMEM((8, 480, 512), jnp.bfloat16),
            pltpu.VMEM((8, 128, 512), jnp.bfloat16),
            pltpu.VMEM((4, 2, 256, 160), jnp.bfloat16),
            pltpu.SemaphoreType.DMA((COPIES,)),
            pltpu.SemaphoreType.DMA((COPIES,)),
            pltpu.SemaphoreType.DMA((4,)),
        ],
        compiler_params=pltpu.CompilerParams(
            collective_id=0, has_side_effects=True, vmem_limit_bytes=63 * 2**20),
        name="experts",
    )(tokens, meta, gate_weight, up_weight, down_weight)


def solution(mesh):
    placed = (
        P(("dp", "expert"), None),
        P(("dp", "expert"), None),
        P(("dp", "expert"), None),
        P("expert", "dp", None),
        P("expert", "dp", None),
        P("expert", None, "dp"),
    )
    return jax.shard_map(
        on_device, mesh=mesh, in_specs=placed, out_specs=P(("dp", "expert"), None), check_vma=False
    )
```

```python
import jax
import jax.numpy as jnp
from jax import lax
from jax.experimental import pallas as pl
from jax.experimental.pallas import tpu as pltpu
from jax.sharding import PartitionSpec as P

CAP = 80
MESH = pl.DeviceIdType.MESH
COPIES = 120

def slot(dz, dy):
    return (dz % 4) * 2 + dy


def kernel(tok_hbm, ids_ref, probs_ref, gate_hbm, up_hbm, down_hbm, kept_hbm, peer_hbm,
           gate_buf, up_buf, down_buf, gate_acc, up_acc, rows, hidden, own_tok, peer_tok, meta_ref, peer_meta,
           back, lanes, mix, ssem, rsem, lsem):
    dp = lax.axis_index("dp")
    ex = lax.axis_index("expert")
    core, y, z = dp % 2, (dp // 2) % 2, dp // 4
    x, h = ex // 2, ex % 2

    def device(x_, h_, z_, y_, c_):
        return (z_ * 4 + y_ * 2 + c_, x_ * 2 + h_)

    z_up, z_down = device(x, h, (z + 1) % 4, y, core), device(x, h, (z + 3) % 4, y, core)
    y_in = device(x, h, z, 1 - y, core)
    sibling = device(x, h, z, y, 1 - core)
    y_out = device(x, 1 - h, z, 1 - y, core)
    x_by = [device((x + d) % 4, h, z, y, core) for d in range(4)]

    partners = (z_up, z_down, y_in, sibling, y_out, x_by[1], x_by[2], x_by[3])
    barrier = pltpu.get_barrier_semaphore()
    load_own = pltpu.make_async_copy(tok_hbm, own_tok.at[pl.ds(0, 128), :], lsem.at[3])
    load_own.start()
    meta_ref[pl.ds(0, 2), :] = ids_ref[...].astype(jnp.float32)
    meta_ref[pl.ds(2, 2), :] = probs_ref[...]
    for partner in partners:
        pl.semaphore_signal(barrier, inc=1, device_id=partner, device_id_type=MESH)
    pl.semaphore_wait(barrier, len(partners))

    sends = []
    left = set()

    def send(src, dst, dev):
        i = len(sends)
        copy = pltpu.make_async_remote_copy(
            src_ref=src, dst_ref=dst, send_sem=ssem.at[i], recv_sem=rsem.at[i],
            device_id=dev, device_id_type=MESH)
        copy.start()
        sends.append(copy)
        return i

    def arrive(i, dst):
        pltpu.make_async_remote_copy(
            src_ref=dst, dst_ref=dst, send_sem=ssem.at[i], recv_sem=rsem.at[i],
            device_id=sibling, device_id_type=MESH).wait_recv()

    args = (gate_hbm.at[0], up_hbm.at[0], down_hbm.at[0])
    bufs = (gate_buf, up_buf, down_buf)
    sizes = (256, 256, 1536)
    extra = (48, 48, 256)
    events = {}
    local = []

    def span(ref, lo, hi):
        return ref.at[pl.ds(lo, hi - lo), :]

    def push(m, key, src, r, lo, hi, dev):
        i = send(span(src, lo, hi), span(bufs[m].at[r, core], lo, hi), dev)
        events[m, key] = (i, r, lo, hi)

    def take(m, key, who):
        i, r, lo, hi = events[m, key]
        arrive(i, span(bufs[m].at[r, who], lo, hi))

    def pass_on(m, key):
        i, r, lo, hi = events[m, key]
        take(m, key, core)
        push(m, "s" + key, bufs[m].at[r, core], r, lo, hi, sibling)

    def send_own(m, key):
        r, dev = {"y": (slot(0, 1), y_in), "zu": (slot(3, 0), z_up), "zd": (slot(1, 0), z_down)}[key]
        push(m, key, args[m], r, 0, sizes[m], dev)

    def keep_own(m):
        push(m, "sown", args[m], slot(0, 0), 0, sizes[m], sibling)

    for m in range(3):
        copy = pltpu.make_async_copy(args[m], bufs[m].at[slot(0, 0), core], lsem.at[m])
        copy.start()
        local.append(copy)

    def relay_half(m, key):
        n = sizes[m]
        dz, lo, hi, dev = {"zu": (3, 0, n // 2, z_up), "zd": (1, n // 2, n, z_down)}[key]
        take(m, key, core)
        src = bufs[m].at[slot(dz, 0), core]
        push(m, "2" + key, src, slot(2, 0), lo, hi, dev)
        push(m, "q" + key, src, slot(dz, 1), n - extra[m], n, y_in)
        push(m, "s" + key, src, slot(dz, 0), 0, n, sibling)

    def relay_peer(m):
        n = sizes[m]
        take(m, "y", core)
        src = bufs[m].at[slot(0, 1), core]
        push(m, "yzu", src, slot(3, 1), 0, n - extra[m], z_up)
        push(m, "yzd", src, slot(1, 1), 0, n - extra[m], z_down)
        push(m, "sy", src, slot(0, 1), 0, n, sibling)

    def relay_far(m, key):
        i, r, lo, hi = events[m, key]
        take(m, key, core)
        push(m, "y" + key, bufs[m].at[r, core], slot(2, 1), lo, hi, y_in)
        push(m, "s" + key, bufs[m].at[r, core], r, lo, hi, sibling)

    from_sibling = {
        slot(0, 0): ("sown",), slot(0, 1): ("sy",), slot(3, 0): ("szu",), slot(1, 0): ("szd",),
        slot(2, 0): ("s2zu", "s2zd"), slot(3, 1): ("sqzu", "syzu"), slot(1, 1): ("sqzd", "syzd"),
        slot(2, 1): ("sy2zu", "sy2zd")}

    def whole_slot(m, r):
        if r == slot(0, 0):
            local[m].wait()
        for key in from_sibling[r]:
            take(m, key, 1 - core)

    later = (lax.broadcasted_iota(jnp.int32, (128, 128), 0)
             < lax.broadcasted_iota(jnp.int32, (128, 128), 1)).astype(jnp.bfloat16)
    place = lax.broadcasted_iota(jnp.int32, (CAP, 128), 0).astype(jnp.float32)
    ahead = (lax.broadcasted_iota(jnp.int32, (8, 128), 0) + 1) % 4
    experts = (((x + ahead) % 4) * 2 + h).astype(jnp.float32)

    def route(meta):
        first, second = meta[0:1, :] == experts, meta[1:2, :] == experts
        named = jnp.where(first | second, 1.0, 0.0)
        weight = jnp.where(first, meta[2:3, :], 0.0) + jnp.where(second, meta[3:4, :], 0.0)
        rank = jnp.dot(named.astype(jnp.bfloat16), later, preferred_element_type=jnp.float32)
        picks = [jnp.where(place == rank[b:b + 1, :], named[b:b + 1, :], 0.0) for b in range(4)]
        return picks, [picks[b] * weight[b:b + 1, :] for b in range(4)]

    def dispatch(part, picks, source):
        chosen = jnp.concatenate(picks, axis=0).astype(jnp.bfloat16)

        def block(j, carry):
            cols = pl.ds(pl.multiple_of(j * 512, 512), 512)
            got = jnp.dot(chosen, source[pl.ds(0, 128), cols], preferred_element_type=jnp.float32).astype(jnp.bfloat16)
            for b in range(3):
                lanes[j, pl.ds(b * 160 + part * CAP, CAP), :] = got[b * CAP:(b + 1) * CAP]
            rows[j, pl.ds(480 + part * CAP, CAP), :] = got[3 * CAP:]
            return carry

        lax.fori_loop(0, 8, block, 0)
        ids = []
        for b in (0, 2, 1):
            at = pl.ds(b * 160 + part * CAP, CAP)
            ids.append((send(lanes.at[:, at, :], rows.at[:, at, :], x_by[b + 1]), at))
        return ids

    def block_of(r):
        return ((z + r // 2) % 4) * 2 + (y + r % 2) % 2

    accs = (gate_acc, up_acc)

    def clear():
        gate_acc[...] = jnp.zeros_like(gate_acc)
        up_acc[...] = jnp.zeros_like(up_acc)

    def project(m, r):
        whole_slot(m, r)
        chip = block_of(r)
        for n in range(2):
            at = pl.ds(n * 320, 320)
            accs[m][at, :] += jnp.dot(
                rows[chip, at, :], bufs[m][r].reshape(512, 1536), preferred_element_type=jnp.float32)

    def project_last(r):
        whole_slot(1, r)

        def tile(n, carry):
            cols = pl.ds(pl.multiple_of(n * 512, 512), 512)
            got = jnp.dot(
                rows[block_of(r)], up_buf[r, :, :, cols].reshape(512, 512), preferred_element_type=jnp.float32)
            hidden[:, cols] = (gate_acc[:, cols] * (up_acc[:, cols] + got)).astype(jnp.bfloat16)
            return carry

        lax.fori_loop(0, 3, tile, 0)

    def activate():
        def tile(n, carry):
            at = pl.ds(pl.multiple_of(n * 32, 32), 32)
            g = gate_acc[at, :]
            gate_acc[at, :] = g / (1.0 + jnp.exp(-g))
            return carry

        lax.fori_loop(0, 20, tile, 0)

    homes = (own_tok, peer_tok, back)
    returns = {}

    def expand(g):
        whole_slot(2, g)

        for n in range(2):
            rows[g, :, pl.ds(n * 256, 256)] = jnp.dot(
                hidden[...], down_buf[g, n], preferred_element_type=jnp.float32).astype(jnp.bfloat16)
        returns[g] = []
        for b in (0, 2, 1):
            dst = homes[b].at[:, pl.ds(g * 512, 512)]
            returns[g].append((send(rows.at[g, pl.ds(b * 160, 160), :], dst, x_by[3 - b]), dst))

    parts = {}
    dispatched, keeps = [], []

    def columns(g):
        return pl.ds(pl.multiple_of(block_of(g) * 512, 512), 512)


    def combine(g):
        for i, dst in returns[g]:
            arrive(i, dst)
        total = 0.0
        for b in range(4):
            block = homes[b][:, pl.ds(g * 512, 512)] if b < 3 else rows[g, pl.ds(480, 160), :]
            for half in range(2):
                total = total + jnp.dot(mix[b, half], block, preferred_element_type=jnp.float32)
        kept = (pl.ds((g // 2) * 128, 128), pl.ds((g % 2) * 512, 512))
        gate_acc[kept] = total[:128]
        copy = pltpu.make_async_copy(gate_acc.at[kept], kept_hbm.at[:, columns(g)], lsem.at[4 + g])
        copy.start()
        keeps.append(copy)
        if not parts:
            for i, at in dispatched:
                sends[i].wait_send()
                left.add(i)
        lanes[g, pl.ds(0, 128), :] = total[128:].astype(jnp.bfloat16)
        parts[g] = send(lanes.at[g, pl.ds(0, 128), :], peer_hbm.at[:, columns(g)], y_out)

    def finish():
        for g in range(8):
            arrive(parts[g], peer_hbm.at[:, columns(g ^ 1)])
        for copy in keeps:
            copy.wait()

    def set_mix(weighed, peer_weighed):
        nothing = jnp.zeros((CAP, 128), jnp.float32)
        for b in range(4):
            whole = jnp.concatenate(
                [jnp.concatenate([weighed[b], nothing], axis=1),
                 jnp.concatenate([nothing, peer_weighed[b]], axis=1)], axis=0).T
            high = whole.astype(jnp.bfloat16)
            mix[b, 0] = high
            mix[b, 1] = (whole - high.astype(jnp.float32)).astype(jnp.bfloat16)

    here, across, up1, down1 = slot(0, 0), slot(0, 1), slot(3, 0), slot(1, 0)
    far, up2, down2, far2 = slot(2, 0), slot(3, 1), slot(1, 1), slot(2, 1)

    meta_id = send(meta_ref, peer_meta, y_out)
    tok_id = send(tok_hbm, peer_tok.at[pl.ds(0, 128), :], y_out)
    send_own(0, "zd")
    send_own(0, "zu")
    send_own(1, "y")
    load_own.wait()
    picks, weighed = route(meta_ref[...])
    dispatched += dispatch(0, picks, own_tok)
    clear()
    send_own(1, "zd")
    send_own(0, "y")
    keep_own(1)
    send_own(1, "zu")
    relay_half(0, "zd")
    relay_half(0, "zu")
    relay_half(1, "zu")
    arrive(meta_id, peer_meta)
    arrive(tok_id, peer_tok.at[pl.ds(0, 128), :])
    peer_picks, peer_weighed = route(peer_meta[...])
    dispatched += dispatch(1, peer_picks, peer_tok)
    set_mix(weighed, peer_weighed)
    relay_half(1, "zd")
    relay_far(0, "2zd")
    relay_peer(0)
    pass_on(0, "qzu")
    relay_far(0, "2zu")
    relay_far(1, "2zd")
    relay_peer(1)
    keep_own(2)
    keep_own(0)
    for i, at in dispatched:
        arrive(i, rows.at[:, at, :])
    relay_far(1, "2zu")
    project(0, here)
    project(1, far)
    pass_on(0, "y2zu")
    project(1, up1)
    project(1, across)
    pass_on(1, "qzd")
    project(0, up1)
    project(1, down1)
    pass_on(0, "yzd")
    pass_on(0, "yzu")
    send_own(2, "zd")
    project(1, here)
    pass_on(1, "y2zd")
    send_own(2, "y")
    pass_on(0, "qzd")
    pass_on(0, "y2zd")
    pass_on(1, "qzu")
    project(0, far)
    project(0, up2)
    send_own(2, "zu")
    project(0, across)
    project(0, down2)
    project(0, far2)
    pass_on(1, "y2zu")
    project(0, down1)
    pass_on(1, "yzu")
    pass_on(1, "yzd")
    project(1, far2)
    project(1, up2)
    activate()
    project_last(down2)
    expand(here)
    relay_half(2, "zd")
    relay_half(2, "zu")
    relay_peer(2)
    expand(down1)
    expand(up1)
    relay_far(2, "2zd")
    expand(across)
    relay_far(2, "2zu")
    pass_on(2, "yzd")
    expand(far)
    combine(across)
    pass_on(2, "qzd")
    pass_on(2, "qzu")
    expand(down2)
    pass_on(2, "y2zu")
    combine(down1)
    pass_on(2, "y2zd")
    combine(far)
    combine(here)
    combine(up1)
    expand(far2)
    pass_on(2, "yzu")
    combine(down2)
    expand(up2)
    combine(far2)
    combine(up2)
    finish()
    for i, copy in enumerate(sends):
        if i not in left:
            copy.wait_send()


def on_device(tokens, expert_ids, gate_probs, gate_weight, up_weight, down_weight):
    hbm, vmem = pl.BlockSpec(memory_space=pltpu.HBM), pl.BlockSpec(memory_space=pltpu.VMEM)
    kept, peer = pl.pallas_call(
        kernel,
        out_shape=(jax.ShapeDtypeStruct((128, 4096), jnp.float32), jax.ShapeDtypeStruct((128, 4096), jnp.bfloat16)),
        in_specs=[hbm, vmem, vmem, hbm, hbm, hbm],
        out_specs=(hbm, hbm),
        scratch_shapes=[
            pltpu.VMEM((8, 2, 256, 1536), jnp.bfloat16),
            pltpu.VMEM((8, 2, 256, 1536), jnp.bfloat16),
            pltpu.VMEM((8, 2, 1536, 256), jnp.bfloat16),
            pltpu.VMEM((640, 1536), jnp.float32),
            pltpu.VMEM((640, 1536), jnp.float32),
            pltpu.VMEM((8, 640, 512), jnp.bfloat16),
            pltpu.VMEM((640, 1536), jnp.bfloat16),
            pltpu.VMEM((160, 4096), jnp.bfloat16),
            pltpu.VMEM((160, 4096), jnp.bfloat16),
            pltpu.VMEM((8, 128), jnp.float32),
            pltpu.VMEM((8, 128), jnp.float32),
            pltpu.VMEM((160, 4096), jnp.bfloat16),
            pltpu.VMEM((8, 480, 512), jnp.bfloat16),
            pltpu.VMEM((4, 2, 256, 160), jnp.bfloat16),
            pltpu.SemaphoreType.DMA((COPIES,)),
            pltpu.SemaphoreType.DMA((COPIES,)),
            pltpu.SemaphoreType.DMA((12,)),
        ],
        compiler_params=pltpu.CompilerParams(
            collective_id=0, has_side_effects=True, vmem_limit_bytes=63 * 2**20),
        name="experts",
    )(tokens, expert_ids.T, gate_probs.T, gate_weight, up_weight, down_weight)
    return (kept + peer.astype(jnp.float32)).astype(jnp.bfloat16)


def solution(mesh):
    placed = (
        P(("dp", "expert"), None),
        P(("dp", "expert"), None),
        P(("dp", "expert"), None),
        P("expert", "dp", None),
        P("expert", "dp", None),
        P("expert", None, "dp"),
    )
    return jax.shard_map(
        on_device, mesh=mesh, in_specs=placed, out_specs=P(("dp", "expert"), None), check_vma=False
    )
```

```python
import jax
import jax.numpy as jnp
from jax import lax
from jax.experimental import pallas as pl
from jax.experimental.pallas import tpu as pltpu
from jax.sharding import PartitionSpec as P

CAP = 80
MESH = pl.DeviceIdType.MESH
COPIES = 120

def slot(dz, dy):
    return (dz % 4) * 2 + dy


def kernel(tok_hbm, ids_ref, probs_ref, gate_hbm, up_hbm, down_hbm, kept_ref, peer_ref,
           gate_buf, up_buf, down_buf, gate_acc, up_acc, rows, hidden, own_tok, peer_tok, meta_ref, peer_meta,
           back, lanes, mix, ssem, rsem, lsem):
    dp = lax.axis_index("dp")
    ex = lax.axis_index("expert")
    core, y, z = dp % 2, (dp // 2) % 2, dp // 4
    x, h = ex // 2, ex % 2

    def device(x_, h_, z_, y_, c_):
        return (z_ * 4 + y_ * 2 + c_, x_ * 2 + h_)

    z_up, z_down = device(x, h, (z + 1) % 4, y, core), device(x, h, (z + 3) % 4, y, core)
    y_in = device(x, h, z, 1 - y, core)
    sibling = device(x, h, z, y, 1 - core)
    y_out = device(x, 1 - h, z, 1 - y, core)
    x_by = [device((x + d) % 4, h, z, y, core) for d in range(4)]

    partners = (z_up, z_down, y_in, sibling, y_out, x_by[1], x_by[2], x_by[3])
    barrier = pltpu.get_barrier_semaphore()
    load_own = pltpu.make_async_copy(tok_hbm, own_tok.at[pl.ds(0, 128), :], lsem.at[3])
    load_own.start()
    meta_ref[pl.ds(0, 2), :] = ids_ref[...].astype(jnp.float32)
    meta_ref[pl.ds(2, 2), :] = probs_ref[...]
    for partner in partners:
        pl.semaphore_signal(barrier, inc=1, device_id=partner, device_id_type=MESH)
    pl.semaphore_wait(barrier, len(partners))

    sends = []
    left = set()

    def send(src, dst, dev):
        i = len(sends)
        copy = pltpu.make_async_remote_copy(
            src_ref=src, dst_ref=dst, send_sem=ssem.at[i], recv_sem=rsem.at[i],
            device_id=dev, device_id_type=MESH)
        copy.start()
        sends.append(copy)
        return i

    def arrive(i, dst):
        pltpu.make_async_remote_copy(
            src_ref=dst, dst_ref=dst, send_sem=ssem.at[i], recv_sem=rsem.at[i],
            device_id=sibling, device_id_type=MESH).wait_recv()

    args = (gate_hbm.at[0], up_hbm.at[0], down_hbm.at[0])
    bufs = (gate_buf, up_buf, down_buf)
    sizes = (256, 256, 1536)
    extra = (48, 48, 256)
    events = {}
    local = []

    def span(ref, lo, hi):
        return ref.at[pl.ds(lo, hi - lo), :]

    def push(m, key, src, r, lo, hi, dev):
        i = send(span(src, lo, hi), span(bufs[m].at[r, core], lo, hi), dev)
        events[m, key] = (i, r, lo, hi)

    def take(m, key, who):
        i, r, lo, hi = events[m, key]
        arrive(i, span(bufs[m].at[r, who], lo, hi))

    def pass_on(m, key):
        i, r, lo, hi = events[m, key]
        take(m, key, core)
        push(m, "s" + key, bufs[m].at[r, core], r, lo, hi, sibling)

    def send_own(m, key):
        r, dev = {"y": (slot(0, 1), y_in), "zu": (slot(3, 0), z_up), "zd": (slot(1, 0), z_down)}[key]
        push(m, key, args[m], r, 0, sizes[m], dev)

    def keep_own(m):
        push(m, "sown", args[m], slot(0, 0), 0, sizes[m], sibling)

    for m in range(3):
        copy = pltpu.make_async_copy(args[m], bufs[m].at[slot(0, 0), core], lsem.at[m])
        copy.start()
        local.append(copy)

    def relay_half(m, key):
        n = sizes[m]
        dz, lo, hi, dev = {"zu": (3, 0, n // 2, z_up), "zd": (1, n // 2, n, z_down)}[key]
        take(m, key, core)
        src = bufs[m].at[slot(dz, 0), core]
        push(m, "2" + key, src, slot(2, 0), lo, hi, dev)
        push(m, "q" + key, src, slot(dz, 1), n - extra[m], n, y_in)
        push(m, "s" + key, src, slot(dz, 0), 0, n, sibling)

    def relay_peer(m):
        n = sizes[m]
        take(m, "y", core)
        src = bufs[m].at[slot(0, 1), core]
        push(m, "yzu", src, slot(3, 1), 0, n - extra[m], z_up)
        push(m, "yzd", src, slot(1, 1), 0, n - extra[m], z_down)
        push(m, "sy", src, slot(0, 1), 0, n, sibling)

    def relay_far(m, key):
        i, r, lo, hi = events[m, key]
        take(m, key, core)
        push(m, "y" + key, bufs[m].at[r, core], slot(2, 1), lo, hi, y_in)
        push(m, "s" + key, bufs[m].at[r, core], r, lo, hi, sibling)

    from_sibling = {
        slot(0, 0): ("sown",), slot(0, 1): ("sy",), slot(3, 0): ("szu",), slot(1, 0): ("szd",),
        slot(2, 0): ("s2zu", "s2zd"), slot(3, 1): ("sqzu", "syzu"), slot(1, 1): ("sqzd", "syzd"),
        slot(2, 1): ("sy2zu", "sy2zd")}

    def whole_slot(m, r):
        if r == slot(0, 0):
            local[m].wait()
        for key in from_sibling[r]:
            take(m, key, 1 - core)

    later = (lax.broadcasted_iota(jnp.int32, (128, 128), 0)
             < lax.broadcasted_iota(jnp.int32, (128, 128), 1)).astype(jnp.bfloat16)
    place = lax.broadcasted_iota(jnp.int32, (CAP, 128), 0).astype(jnp.float32)
    ahead = (lax.broadcasted_iota(jnp.int32, (8, 128), 0) + 1) % 4
    experts = (((x + ahead) % 4) * 2 + h).astype(jnp.float32)

    def route(meta):
        first, second = meta[0:1, :] == experts, meta[1:2, :] == experts
        named = jnp.where(first | second, 1.0, 0.0)
        weight = jnp.where(first, meta[2:3, :], 0.0) + jnp.where(second, meta[3:4, :], 0.0)
        rank = jnp.dot(named.astype(jnp.bfloat16), later, preferred_element_type=jnp.float32)
        picks = [jnp.where(place == rank[b:b + 1, :], named[b:b + 1, :], 0.0) for b in range(4)]
        return picks, [picks[b] * weight[b:b + 1, :] for b in range(4)]

    def dispatch(part, picks, source):
        chosen = jnp.concatenate(picks, axis=0).astype(jnp.bfloat16)

        def block(j, carry):
            cols = pl.ds(pl.multiple_of(j * 512, 512), 512)
            got = jnp.dot(chosen, source[pl.ds(0, 128), cols], preferred_element_type=jnp.float32).astype(jnp.bfloat16)
            for b in range(3):
                lanes[j, pl.ds(b * 160 + part * CAP, CAP), :] = got[b * CAP:(b + 1) * CAP]
            rows[j, pl.ds(480 + part * CAP, CAP), :] = got[3 * CAP:]
            return carry

        lax.fori_loop(0, 8, block, 0)
        ids = []
        for b in (0, 2, 1):
            at = pl.ds(b * 160 + part * CAP, CAP)
            ids.append((send(lanes.at[:, at, :], rows.at[:, at, :], x_by[b + 1]), at))
        return ids

    def block_of(r):
        return ((z + r // 2) % 4) * 2 + (y + r % 2) % 2

    accs = (gate_acc, up_acc)

    def clear():
        gate_acc[...] = jnp.zeros_like(gate_acc)
        up_acc[...] = jnp.zeros_like(up_acc)

    def project(m, r):
        whole_slot(m, r)
        chip = block_of(r)
        for n in range(2):
            at = pl.ds(n * 320, 320)
            accs[m][at, :] += jnp.dot(
                rows[chip, at, :], bufs[m][r].reshape(512, 1536), preferred_element_type=jnp.float32)

    def project_last(r):
        whole_slot(1, r)

        def tile(n, carry):
            cols = pl.ds(pl.multiple_of(n * 512, 512), 512)
            got = jnp.dot(
                rows[block_of(r)], up_buf[r, :, :, cols].reshape(512, 512), preferred_element_type=jnp.float32)
            hidden[:, cols] = (gate_acc[:, cols] * (up_acc[:, cols] + got)).astype(jnp.bfloat16)
            return carry

        lax.fori_loop(0, 3, tile, 0)

    def activate():
        def tile(n, carry):
            at = pl.ds(pl.multiple_of(n * 32, 32), 32)
            g = gate_acc[at, :]
            gate_acc[at, :] = g / (1.0 + jnp.exp(-g))
            return carry

        lax.fori_loop(0, 20, tile, 0)

    homes = (own_tok, peer_tok, back)
    returns = {}

    def expand(g):
        whole_slot(2, g)

        for n in range(2):
            rows[g, :, pl.ds(n * 256, 256)] = jnp.dot(
                hidden[...], down_buf[g, n], preferred_element_type=jnp.float32).astype(jnp.bfloat16)
        returns[g] = []
        for b in (0, 2, 1):
            dst = homes[b].at[:, pl.ds(g * 512, 512)]
            returns[g].append((send(rows.at[g, pl.ds(b * 160, 160), :], dst, x_by[3 - b]), dst))

    parts = {}
    dispatched = []

    def columns(g):
        return pl.ds(pl.multiple_of(block_of(g) * 512, 512), 512)


    def combine(g):
        for i, dst in returns[g]:
            arrive(i, dst)
        total = 0.0
        for b in range(4):
            block = homes[b][:, pl.ds(g * 512, 512)] if b < 3 else rows[g, pl.ds(480, 160), :]
            for half in range(2):
                total = total + jnp.dot(mix[b, half], block, preferred_element_type=jnp.float32)
        kept_ref[:, columns(g)] = total[:128].astype(jnp.bfloat16)
        if not parts:
            for i, at in dispatched:
                sends[i].wait_send()
                left.add(i)
        lanes[g, pl.ds(0, 128), :] = total[128:].astype(jnp.bfloat16)
        parts[g] = send(lanes.at[g, pl.ds(0, 128), :], peer_ref.at[:, columns(g)], y_out)

    def finish():
        for g in range(8):
            arrive(parts[g], peer_ref.at[:, columns(g ^ 1)])

    def set_mix(weighed, peer_weighed):
        nothing = jnp.zeros((CAP, 128), jnp.float32)
        for b in range(4):
            whole = jnp.concatenate(
                [jnp.concatenate([weighed[b], nothing], axis=1),
                 jnp.concatenate([nothing, peer_weighed[b]], axis=1)], axis=0).T
            high = whole.astype(jnp.bfloat16)
            mix[b, 0] = high
            mix[b, 1] = (whole - high.astype(jnp.float32)).astype(jnp.bfloat16)

    here, across, up1, down1 = slot(0, 0), slot(0, 1), slot(3, 0), slot(1, 0)
    far, up2, down2, far2 = slot(2, 0), slot(3, 1), slot(1, 1), slot(2, 1)

    meta_id = send(meta_ref, peer_meta, y_out)
    tok_id = send(tok_hbm, peer_tok.at[pl.ds(0, 128), :], y_out)
    send_own(0, "zd")
    send_own(0, "zu")
    send_own(1, "y")
    load_own.wait()
    picks, weighed = route(meta_ref[...])
    dispatched += dispatch(0, picks, own_tok)
    clear()
    send_own(1, "zd")
    send_own(0, "y")
    keep_own(1)
    send_own(1, "zu")
    relay_half(0, "zd")
    relay_half(0, "zu")
    relay_half(1, "zu")
    arrive(meta_id, peer_meta)
    arrive(tok_id, peer_tok.at[pl.ds(0, 128), :])
    peer_picks, peer_weighed = route(peer_meta[...])
    dispatched += dispatch(1, peer_picks, peer_tok)
    set_mix(weighed, peer_weighed)
    relay_half(1, "zd")
    relay_far(0, "2zd")
    relay_peer(0)
    pass_on(0, "qzu")
    relay_far(0, "2zu")
    relay_far(1, "2zd")
    relay_peer(1)
    keep_own(2)
    keep_own(0)
    for i, at in dispatched:
        arrive(i, rows.at[:, at, :])
    relay_far(1, "2zu")
    project(0, here)
    project(1, far)
    pass_on(0, "y2zu")
    project(1, up1)
    project(1, across)
    pass_on(1, "qzd")
    project(0, up1)
    project(1, down1)
    pass_on(0, "yzd")
    pass_on(0, "yzu")
    send_own(2, "zd")
    project(1, here)
    pass_on(1, "y2zd")
    send_own(2, "y")
    pass_on(0, "qzd")
    pass_on(0, "y2zd")
    pass_on(1, "qzu")
    project(0, far)
    project(0, up2)
    send_own(2, "zu")
    project(0, across)
    project(0, down2)
    project(0, far2)
    pass_on(1, "y2zu")
    project(0, down1)
    pass_on(1, "yzu")
    pass_on(1, "yzd")
    project(1, far2)
    project(1, up2)
    activate()
    project_last(down2)
    expand(here)
    relay_half(2, "zd")
    relay_half(2, "zu")
    relay_peer(2)
    expand(down1)
    expand(up1)
    relay_far(2, "2zd")
    expand(across)
    relay_far(2, "2zu")
    pass_on(2, "yzd")
    expand(far)
    combine(across)
    pass_on(2, "qzd")
    pass_on(2, "qzu")
    expand(down2)
    pass_on(2, "y2zu")
    combine(down1)
    pass_on(2, "y2zd")
    combine(far)
    combine(here)
    combine(up1)
    expand(far2)
    pass_on(2, "yzu")
    combine(down2)
    expand(up2)
    combine(far2)
    combine(up2)
    finish()
    for i, copy in enumerate(sends):
        if i not in left:
            copy.wait_send()


def on_device(tokens, expert_ids, gate_probs, gate_weight, up_weight, down_weight):
    hbm, vmem = pl.BlockSpec(memory_space=pltpu.HBM), pl.BlockSpec(memory_space=pltpu.VMEM)
    kept, peer = pl.pallas_call(
        kernel,
        out_shape=(jax.ShapeDtypeStruct((128, 4096), jnp.bfloat16), jax.ShapeDtypeStruct((128, 4096), jnp.bfloat16)),
        in_specs=[hbm, vmem, vmem, hbm, hbm, hbm],
        out_specs=(vmem, vmem),
        scratch_shapes=[
            pltpu.VMEM((8, 2, 256, 1536), jnp.bfloat16),
            pltpu.VMEM((8, 2, 256, 1536), jnp.bfloat16),
            pltpu.VMEM((8, 2, 1536, 256), jnp.bfloat16),
            pltpu.VMEM((640, 1536), jnp.float32),
            pltpu.VMEM((640, 1536), jnp.float32),
            pltpu.VMEM((8, 640, 512), jnp.bfloat16),
            pltpu.VMEM((640, 1536), jnp.bfloat16),
            pltpu.VMEM((160, 4096), jnp.bfloat16),
            pltpu.VMEM((160, 4096), jnp.bfloat16),
            pltpu.VMEM((8, 128), jnp.float32),
            pltpu.VMEM((8, 128), jnp.float32),
            pltpu.VMEM((160, 4096), jnp.bfloat16),
            pltpu.VMEM((8, 480, 512), jnp.bfloat16),
            pltpu.VMEM((4, 2, 256, 160), jnp.bfloat16),
            pltpu.SemaphoreType.DMA((COPIES,)),
            pltpu.SemaphoreType.DMA((COPIES,)),
            pltpu.SemaphoreType.DMA((4,)),
        ],
        compiler_params=pltpu.CompilerParams(
            collective_id=0, has_side_effects=True, vmem_limit_bytes=63 * 2**20),
        name="experts",
    )(tokens, expert_ids.T, gate_probs.T, gate_weight, up_weight, down_weight)
    return (kept.astype(jnp.float32) + peer.astype(jnp.float32)).astype(jnp.bfloat16)


def solution(mesh):
    placed = (
        P(("dp", "expert"), None),
        P(("dp", "expert"), None),
        P(("dp", "expert"), None),
        P("expert", "dp", None),
        P("expert", "dp", None),
        P("expert", None, "dp"),
    )
    return jax.shard_map(
        on_device, mesh=mesh, in_specs=placed, out_specs=P(("dp", "expert"), None), check_vma=False
    )
```
